32 devices in a mesh: row: 4 (over y, x), col: 8 (over z, core).
Axes of the slice: x: 2, y: 2, z: 4, core: 2. Of those that a mesh axis runs over, the one named last changes fastest.
Arguments:
- vectors: bfloat16 [512, 8192], P('row', 'col'), may hold values from -6 to 6
- factor_tiles: bfloat16 [32, 24, 256, 256], P('row', 'col'), may hold values from -0.109375 to 0.109375
- tile_columns: int32 [32, 24], P('row', 'col'), may hold values from 0 to 31, as said below
- live_counts: int32 [32, 8], P('row', 'col'), may hold values from 0 to 3, as said below
Outputs:
- applied: float32 [512, 8192], P('row', 'col')
The draws below stay inside these ranges and needn't reach their ends.
Inputs may be any that keep to these rules, and one draw needn't show every extreme that they name: `tile_columns`: slot s holds a tile column in [(s // 3) * 4, (s // 3 + 1) * 4); the slots of one row tile name distinct columns; a live slot's column is at most its row tile; the row tile's own column is always live, in the first slot of its group. `live_counts`: counts never exceed the columns allowed in that group, so the upper right region of groups is empty. In group 0 every row tile i >= 2 has exactly 3 live slots.
All inputs are finite; a program needn't handle non-finite values.
Results may differ from the reference program's by a relative error of at most 0.002.
Values may be sent and summed in bfloat16 or wider, within the bound.
A program may use at most 64 MiB of HBM per device.

```python
import jax
import jax.numpy as jnp
from jax import lax

TILE = 256
CT = 4
K_C = 3
NV = 512
NB = 32
SLOTS = 24
ORDER = 8192
N_COL = 8


def draw_tile_columns(key, part):
    row_ids = jnp.arange(NB, dtype=jnp.int32)[:, None, None]
    group_ids = jnp.arange(N_COL, dtype=jnp.int32)[None, :, None]
    local_ids = jnp.arange(CT, dtype=jnp.int32)[None, None, :]
    reach = row_ids - group_ids * CT
    noise = jax.random.randint(key, (NB, N_COL, CT), 0, 4096, dtype=jnp.int32)
    scores = noise * CT + local_ids
    scores = jnp.where(local_ids > reach, scores + 4096 * CT * 2, scores)
    scores = jnp.where(local_ids == reach, -1, scores)
    order = jnp.argsort(scores, axis=2, stable=True)[:, :, :K_C]
    return (order + group_ids * CT).reshape(NB, SLOTS).astype(jnp.int32)


def draw_live_counts(key, part):
    row_ids = jnp.arange(NB, dtype=jnp.int32)[:, None]
    group_ids = jnp.arange(N_COL, dtype=jnp.int32)[None, :]
    allowed = jnp.clip(row_ids - group_ids * CT + 1, 0, CT)
    chosen = jax.random.randint(key, (NB, N_COL), 1, K_C + 1, dtype=jnp.int32)
    chosen = jnp.where(group_ids == 0, K_C, chosen)
    return jnp.minimum(chosen, allowed).astype(jnp.int32)


def block_scale(rng, extent, cuts, low, high):
    loudness, own = 1.0, jax.random.fold_in(rng, 6)
    for axis_at, shards_of in cuts:
        heights = jnp.exp(jax.random.uniform(jax.random.fold_in(own, axis_at), (shards_of,), jnp.float32, low / len(cuts), high / len(cuts)))
        loudness = loudness * jnp.repeat(heights, extent[axis_at] // shards_of).reshape([-1 if axis == axis_at else 1 for axis in range(len(extent))])
    return loudness


def scatter_about(rng, extent, spread, most, split=(), held_as=jnp.bfloat16):
    values = spread * jax.random.normal(rng, extent, jnp.float32)
    if split:
        values = values * block_scale(rng, extent, split, -0.22, 0.18)
    return jnp.clip(values, -most, most).astype(held_as)


def setup_inputs(seed: int = 0) -> dict:
    arg_keys = jax.random.split(jax.random.key(seed), 5)
    vectors = scatter_about(arg_keys[0], (NV, ORDER), 1.0, 6.0, ((0, 4), (1, 8)))
    factor_tiles = scatter_about(arg_keys[1], (NB, SLOTS, TILE, TILE), (TILE * K_C * N_COL // 2) ** -0.5, 0.109375, ((0, 4), (1, 8)))
    tile_columns = draw_tile_columns(jax.random.fold_in(arg_keys[4], 71), 0)
    live_counts = draw_live_counts(jax.random.fold_in(arg_keys[4], 71), 0)
    return {"vectors": vectors, "factor_tiles": factor_tiles, "tile_columns": tile_columns, "live_counts": live_counts}


def reference(vectors, factor_tiles, tile_columns, live_counts):
    slot_ids = jnp.arange(SLOTS, dtype=jnp.int32)
    live_mask = ((slot_ids % K_C)[None, :] < jnp.repeat(live_counts, K_C, axis=1)).astype(jnp.float32)
    blocks = vectors.reshape(NV, NB, TILE)

    def forward_row(index):
        picked = jnp.take(blocks, tile_columns[index], axis=1).astype(jnp.float32)
        picked = picked * live_mask[index][None, :, None]
        return jnp.einsum("sab,vsb->va", factor_tiles[index].astype(jnp.float32), picked,
                          precision=lax.Precision.HIGHEST)

    row_list = jnp.arange(NB, dtype=jnp.int32)
    rows_out = lax.map(forward_row, row_list)
    rowvals = jnp.transpose(rows_out, (1, 0, 2)).astype(jnp.bfloat16)

    def backward_row(total, index):
        weights = rowvals[:, index].astype(jnp.float32)
        contrib = jnp.einsum("sab,va->svb", factor_tiles[index].astype(jnp.float32), weights,
                             precision=lax.Precision.HIGHEST)
        contrib = contrib * live_mask[index][:, None, None]
        total = total.at[:, tile_columns[index]].add(jnp.transpose(contrib, (1, 0, 2)))
        return total, None

    start_total = jnp.zeros((NV, NB, TILE), jnp.float32)
    total, unused = lax.scan(backward_row, start_total, row_list)
    return total.reshape(NV, NB * TILE)
```

```python
import functools

import jax
import jax.numpy as jnp
from jax import lax
from jax.experimental import pallas as pl
from jax.experimental.pallas import tpu as pltpu
from jax.sharding import PartitionSpec as P

LANES = 128
GROUP = 16
PEAK = 32000.0
MESH = pl.DeviceIdType.MESH


def xor(a, b, size):
    both, bit = 0, 1
    while bit < size:
        both = both + bit * ((a // bit) % 2) * ((b // bit) % 2)
        bit *= 2
    return a + b - 2 * both


def encode(value, ref):
    rows, width = value.shape
    most = jnp.full((GROUP, LANES), 1e-30, jnp.float32)
    for at in range(width // LANES):
        part = jnp.abs(value[:, at * LANES:(at + 1) * LANES])
        most = jnp.maximum(most, jnp.max(part.reshape(rows // GROUP, GROUP, LANES), axis=0))
    power = jnp.ceil(jnp.log2(most))
    scale = jnp.tile(jnp.exp2(-power) * PEAK, (rows // GROUP, 1))
    for at in range(width // LANES):
        coded = jnp.round(value[:, at * LANES:(at + 1) * LANES] * scale)
        ref[at * rows:(at + 1) * rows, :] = coded.astype(jnp.int32).astype(jnp.int16)
    ref[rows * width // LANES:, :] = power.astype(jnp.int32).astype(jnp.int16)


def decode(ref, rows, width):
    power = ref[rows * width // LANES:, :].astype(jnp.int32).astype(jnp.float32)
    scale = jnp.tile(jnp.exp2(power) * (1.0 / PEAK), (rows // GROUP, 1))
    parts = [
        ref[at * rows:(at + 1) * rows, :].astype(jnp.int32).astype(jnp.float32) * scale
        for at in range(width // LANES)
    ]
    return jnp.concatenate(parts, axis=1)


def kernel(
    dims, cols_ref, counts_ref, v_hbm, f_hbm, out_ref,
    v_all, f_all, dense, own, pair_out, pair_in, held, chain_out, chain_in, cross_in, rowvals, part_out, part_in,
    load_sem, v_send, v_recv, pair_send, pair_recv, chain_send, chain_recv, cross_recv,
    far_send, far_recv, near_send, near_recv, part_send, part_recv,
):
    n_row, n_col, n_tiles, n_slots, tile, col_tiles, subs = dims
    n_pair = n_col // 2
    n_vec, width = out_ref.shape
    pieces, rows = n_row * subs, n_vec // subs
    half = n_tiles // 2 * tile

    me_row, me_col = lax.axis_index("row"), lax.axis_index("col")
    pair, core = me_col // 2, me_col % 2
    partner = pair * 2 + 1 - core

    def last_pair(row):
        return jnp.minimum(n_pair - 1, ((row + 1) * n_tiles - 1) // (2 * col_tiles))

    last = last_pair(me_row)
    middle = last // 2
    left = pair <= middle
    active = pair <= last
    solo = last == 0
    center = jnp.logical_and(jnp.logical_or(pair == middle, pair == middle + 1), last > 0)
    depth = jnp.where(left, pair, last - pair)
    spread = jnp.where(left, middle - pair, pair - middle - 1)
    has_outer = depth > 0
    outer = jnp.where(left, pair - 1, pair + 1)
    inner = jnp.where(left, pair + 1, pair - 1)
    outer_col, inner_col = outer * 2 + core, inner * 2 + core
    meet = jnp.where(solo, 0, 1 + jnp.maximum(middle, last - middle - 1))
    total_lag = meet + 1 + spread
    final_lag = total_lag + 1

    load_v = pltpu.make_async_copy(v_hbm, v_all.at[0], load_sem.at[0])
    load_f = pltpu.make_async_copy(f_hbm, f_all, load_sem.at[1])
    load_v.start()
    load_f.start()

    barrier = pltpu.get_barrier_semaphore()
    for k in range(1, n_row):
        pl.semaphore_signal(barrier, inc=1, device_id=(xor(me_row, k, n_row), me_col), device_id_type=MESH)
    pl.semaphore_signal(barrier, inc=1, device_id=(me_row, partner), device_id_type=MESH)

    @pl.when(pair > 0)
    def _():
        pl.semaphore_signal(barrier, inc=1, device_id=(me_row, me_col - 2), device_id_type=MESH)

    @pl.when(pair < n_pair - 1)
    def _():
        pl.semaphore_signal(barrier, inc=1, device_id=(me_row, me_col + 2), device_id_type=MESH)

    edges = jnp.where(pair > 0, 1, 0) + jnp.where(pair < n_pair - 1, 1, 0)
    pl.semaphore_wait(barrier, n_row + edges)

    def remote(src, dst, send, recv, row, col):
        return pltpu.make_async_remote_copy(
            src_ref=src, dst_ref=dst, send_sem=send, recv_sem=recv, device_id=(row, col), device_id_type=MESH
        )

    def v_copy(k):
        return remote(v_hbm, v_all.at[k], v_send.at[k], v_recv.at[k], xor(me_row, k, n_row), me_col)

    def pair_copy(j):
        return remote(pair_out.at[j], pair_in.at[j], pair_send.at[j], pair_recv.at[j], me_row, partner)

    def chain_copy(j):
        return remote(chain_out.at[j], chain_in.at[j], chain_send.at[j], chain_recv.at[j], me_row, inner_col)

    def cross_copy(j):
        return remote(chain_out.at[j], cross_in.at[j], chain_send.at[j], cross_recv.at[j], me_row, inner_col)

    def far_copy(j):
        return remote(rowvals.at[core, j], rowvals.at[core, j], far_send.at[j], far_recv.at[j], me_row, outer_col)

    def near_copy(j):
        return remote(rowvals.at[core, j], rowvals.at[core, j], near_send.at[j], near_recv.at[j], me_row, partner)

    def part_copy(j):
        return remote(
            part_out.at[j], part_in.at[j], part_send.at[j], part_recv.at[j], xor(me_row, j // subs, n_row), me_col
        )

    for k in range(1, n_row):
        @pl.when(pair <= last_pair(xor(me_row, k, n_row)))
        def _():
            v_copy(k).start()

    load_v.wait()
    load_f.wait()

    @pl.when(active)
    def _():
        @pl.loop(0, n_tiles)
        def _(t):
            at = (t % (n_tiles // 2)) * tile
            zero = jnp.zeros((tile, tile), jnp.bfloat16)
            for c in range(col_tiles):
                value = zero
                for s in range(n_slots):
                    pick = jnp.logical_and(cols_ref[t, s] == me_col * col_tiles + c, s < counts_ref[t, 0])
                    value = jnp.where(pick, f_all[t, s], value)
                dense[t // (n_tiles // 2), pl.ds(pl.multiple_of(at, tile), tile), c * tile:(c + 1) * tile] = value

        @pl.loop(0, pieces + final_lag)
        def _(t):
            def valid(j):
                return jnp.logical_and(j >= 0, j < pieces)

            j_total = t - total_lag
            j_in = t - 1 - depth
            j_out = t - final_lag

            @pl.when(jnp.logical_and(valid(j_total), jnp.logical_not(solo)))
            def _():
                @pl.when(center)
                def _():
                    cross_copy(j_total).wait_recv()
                    total = held[j_total] + decode(cross_in.at[j_total], rows, half)
                    rowvals[core, j_total] = total.astype(jnp.bfloat16)

                @pl.when(jnp.logical_not(center))
                def _():
                    far_copy(j_total).wait_recv()

                @pl.when(has_outer)
                def _():
                    far_copy(j_total).start()

                near_copy(j_total).start()

            @pl.when(valid(j_in))
            def _():
                pair_copy(j_in).wait_recv()
                held[j_in] = own[j_in] + pair_in[j_in]

                @pl.when(has_outer)
                def _():
                    chain_copy(j_in).wait_recv()
                    held[j_in] += decode(chain_in.at[j_in], rows, half)

                @pl.when(solo)
                def _():
                    rowvals[core, j_in] = held[j_in].astype(jnp.bfloat16)
                    near_copy(j_in).start()

                @pl.when(jnp.logical_not(solo))
                def _():
                    encode(held[j_in], chain_out.at[j_in])

                    @pl.when(center)
                    def _():
                        cross_copy(j_in).start()

                    @pl.when(jnp.logical_not(center))
                    def _():
                        chain_copy(j_in).start()

            @pl.when(t < pieces)
            def _():
                k, sub = t // subs, t % subs

                @pl.when(jnp.logical_and(k > 0, sub == 0))
                def _():
                    v_copy(k).wait_recv()

                vec = v_all[k, pl.ds(pl.multiple_of(sub * rows, rows), rows), :]
                dims_nt = (((1,), (1,)), ((), ()))
                pair_out[t] = lax.dot_general(vec, dense[1 - core], dims_nt, preferred_element_type=jnp.float32)
                pair_copy(t).start()
                own[t] = lax.dot_general(vec, dense[core], dims_nt, preferred_element_type=jnp.float32)

            @pl.when(valid(j_out))
            def _():
                near_copy(j_out).wait_recv()
                part = jnp.dot(rowvals[0, j_out], dense[0], preferred_element_type=jnp.float32)
                part += jnp.dot(rowvals[1, j_out], dense[1], preferred_element_type=jnp.float32)

                @pl.when(j_out < subs)
                def _():
                    out_ref[pl.ds(pl.multiple_of(j_out * rows, rows), rows), :] = part

                @pl.when(j_out >= subs)
                def _():
                    encode(part, part_out.at[j_out])
                    part_copy(j_out).start()

    @pl.when(jnp.logical_not(active))
    def _():
        out_ref[...] = jnp.zeros_like(out_ref)

    @pl.loop(subs, pieces)
    def _(j):
        @pl.when(pair <= last_pair(xor(me_row, j // subs, n_row)))
        def _():
            part_copy(j).wait_recv()
            where = pl.ds(pl.multiple_of((j % subs) * rows, rows), rows)
            out_ref[where, :] += decode(part_in.at[j], rows, width)

    for k in range(1, n_row):
        @pl.when(pair <= last_pair(xor(me_row, k, n_row)))
        def _():
            v_copy(k).wait_send()

    @pl.when(active)
    def _():
        @pl.loop(0, pieces)
        def _(j):
            pair_copy(j).wait_send()
            near_copy(j).wait_send()

            @pl.when(jnp.logical_not(solo))
            def _():
                chain_copy(j).wait_send()

            @pl.when(has_outer)
            def _():
                far_copy(j).wait_send()

            @pl.when(j >= subs)
            def _():
                part_copy(j).wait_send()


def per_device(n_row, n_col, vectors, factor_tiles, tile_columns, live_counts):
    n_tiles, n_slots, tile, _ = factor_tiles.shape
    n_vec, width = vectors.shape
    subs = max(1, n_vec // 64)
    pieces, rows = n_row * subs, n_vec // subs
    half = n_tiles // 2 * tile
    coded = rows * half // LANES + GROUP
    coded_out = rows * width // LANES + GROUP
    dma = pltpu.SemaphoreType.DMA
    return pl.pallas_call(
        functools.partial(kernel, (n_row, n_col, n_tiles, n_slots, tile, width // tile, subs)),
        out_shape=jax.ShapeDtypeStruct((n_vec, width), jnp.float32),
        in_specs=[
            pl.BlockSpec(memory_space=pltpu.SMEM),
            pl.BlockSpec(memory_space=pltpu.SMEM),
            pl.BlockSpec(memory_space=pl.ANY),
            pl.BlockSpec(memory_space=pl.ANY),
        ],
        out_specs=pl.BlockSpec(memory_space=pltpu.VMEM),
        scratch_shapes=[
            pltpu.VMEM((n_row, n_vec, width), jnp.bfloat16),
            pltpu.VMEM((n_tiles, n_slots, tile, tile), jnp.bfloat16),
            pltpu.VMEM((2, half, width), jnp.bfloat16),
            pltpu.VMEM((pieces, rows, half), jnp.float32),
            pltpu.VMEM((pieces, rows, half), jnp.float32),
            pltpu.VMEM((pieces, rows, half), jnp.float32),
            pltpu.VMEM((pieces, rows, half), jnp.float32),
            pltpu.VMEM((pieces, coded, LANES), jnp.int16),
            pltpu.VMEM((pieces, coded, LANES), jnp.int16),
            pltpu.VMEM((pieces, coded, LANES), jnp.int16),
            pltpu.VMEM((2, pieces, rows, half), jnp.bfloat16),
            pltpu.VMEM((pieces, coded_out, LANES), jnp.int16),
            pltpu.VMEM((pieces, coded_out, LANES), jnp.int16),
            dma((2,)),
            dma((n_row,)), dma((n_row,)),
            dma((pieces,)), dma((pieces,)),
            dma((pieces,)), dma((pieces,)), dma((pieces,)),
            dma((pieces,)), dma((pieces,)),
            dma((pieces,)), dma((pieces,)),
            dma((pieces,)), dma((pieces,)),
        ],
        compiler_params=pltpu.CompilerParams(
            collective_id=0, has_side_effects=True, vmem_limit_bytes=56 * 1024 * 1024
        ),
    )(tile_columns, live_counts, vectors, factor_tiles)


def solution(mesh):
    in_specs = (P("row", "col"), P("row", "col", None, None), P("row", "col"), P("row", "col"))
    out_specs = P("row", "col")
    body = functools.partial(per_device, mesh.shape["row"], mesh.shape["col"])
    return jax.shard_map(body, mesh=mesh, in_specs=in_specs, out_specs=out_specs, check_vma=False)
```

```python
import functools

import jax
import jax.numpy as jnp
from jax import lax
from jax.experimental import pallas as pl
from jax.experimental.pallas import tpu as pltpu
from jax.sharding import PartitionSpec as P

LANES = 128
GROUP = 16
PEAK = 32000.0
CUTS = 1
LAG_PAIR, LAG_IN, LAG_CROSS, LAG_OUT, LAG_NEAR = 1, 1, 2, 2, 1
MESH = pl.DeviceIdType.MESH


def xor(a, b, size):
    both, bit = 0, 1
    while bit < size:
        both = both + bit * ((a // bit) % 2) * ((b // bit) % 2)
        bit *= 2
    return a + b - 2 * both


def encode(value, ref):
    rows, width = value.shape
    most = jnp.full((GROUP, LANES), 1e-30, jnp.float32)
    for at in range(width // LANES):
        part = jnp.abs(value[:, at * LANES:(at + 1) * LANES])
        most = jnp.maximum(most, jnp.max(part.reshape(rows // GROUP, GROUP, LANES), axis=0))
    power = jnp.ceil(jnp.log2(most))
    scale = jnp.tile(jnp.exp2(-power) * PEAK, (rows // GROUP, 1))
    for at in range(width // LANES):
        coded = jnp.round(value[:, at * LANES:(at + 1) * LANES] * scale)
        ref[at * rows:(at + 1) * rows, :] = coded.astype(jnp.int32).astype(jnp.int16)
    ref[rows * width // LANES:, :] = power.astype(jnp.int32).astype(jnp.int16)


def decode(ref, rows, width):
    power = ref[rows * width // LANES:, :].astype(jnp.int32).astype(jnp.float32)
    scale = jnp.tile(jnp.exp2(power) * (1.0 / PEAK), (rows // GROUP, 1))
    parts = [
        ref[at * rows:(at + 1) * rows, :].astype(jnp.int32).astype(jnp.float32) * scale
        for at in range(width // LANES)
    ]
    return jnp.concatenate(parts, axis=1)


def kernel(
    dims, cols_ref, counts_ref, v_hbm, f_hbm, out_ref,
    v_all, f_all, dense, own, pair_out, pair_in, held, chain_out, chain_in, cross_in, rowvals, part_out, part_in,
    load_sem, v_send, v_recv, pair_send, pair_recv, chain_send, chain_recv, cross_recv,
    far_send, far_recv, near_send, near_recv, part_send, part_recv,
):
    n_row, n_col, n_tiles, n_slots, tile, col_tiles, subs, cuts = dims
    n_pair = n_col // 2
    n_vec, width = out_ref.shape
    pieces, rows = n_row * subs, n_vec // subs
    half = n_tiles // 2 * tile
    thin = rows // cuts

    me_row, me_col = lax.axis_index("row"), lax.axis_index("col")
    pair, core = me_col // 2, me_col % 2
    partner = pair * 2 + 1 - core

    def last_pair(row):
        return jnp.minimum(n_pair - 1, ((row + 1) * n_tiles - 1) // (2 * col_tiles))

    last = last_pair(me_row)
    middle = last // 2
    left = pair <= middle
    active = pair <= last
    solo = last == 0
    center = jnp.logical_and(jnp.logical_or(pair == middle, pair == middle + 1), last > 0)
    depth = jnp.where(left, pair, last - pair)
    spread = jnp.where(left, middle - pair, pair - middle - 1)
    has_outer = depth > 0
    outer = jnp.where(left, pair - 1, pair + 1)
    inner = jnp.where(left, pair + 1, pair - 1)
    outer_col, inner_col = outer * 2 + core, inner * 2 + core
    in_lag = LAG_PAIR + LAG_IN * depth
    meet = LAG_PAIR + LAG_IN * jnp.maximum(middle, last - middle - 1) + LAG_CROSS
    total_lag = meet + LAG_OUT * spread
    final_lag = jnp.where(solo, LAG_PAIR, total_lag) + LAG_NEAR

    def peer_of(j):
        others = j - (subs - 1)
        is_last = j == pieces - 1 if subs > 1 else False
        is_own = jnp.logical_or(others < (1 if subs == 1 else 0), is_last)
        place = 0 if subs == 1 else jnp.where(is_last, subs - 1, j)
        shift = others - 1 if subs == 1 else others
        distance = jnp.where(is_own, 0, 1 + shift // subs)
        return distance, jnp.where(is_own, place, shift % subs), is_own

    def rows_of(place):
        return pl.ds(pl.multiple_of(place * rows, rows), rows)

    load_v = pltpu.make_async_copy(v_hbm, v_all.at[0], load_sem.at[0])
    load_f = pltpu.make_async_copy(f_hbm, f_all, load_sem.at[1])
    load_v.start()
    load_f.start()

    barrier = pltpu.get_barrier_semaphore()
    for k in range(1, n_row):
        pl.semaphore_signal(barrier, inc=1, device_id=(xor(me_row, k, n_row), me_col), device_id_type=MESH)
    pl.semaphore_signal(barrier, inc=1, device_id=(me_row, partner), device_id_type=MESH)

    @pl.when(pair > 0)
    def _():
        pl.semaphore_signal(barrier, inc=1, device_id=(me_row, me_col - 2), device_id_type=MESH)

    @pl.when(pair < n_pair - 1)
    def _():
        pl.semaphore_signal(barrier, inc=1, device_id=(me_row, me_col + 2), device_id_type=MESH)

    def remote(src, dst, send, recv, row, col):
        return pltpu.make_async_remote_copy(
            src_ref=src, dst_ref=dst, send_sem=send, recv_sem=recv, device_id=(row, col), device_id_type=MESH
        )

    def v_copy(k, place):
        return remote(
            v_hbm.at[rows_of(place)], v_all.at[k, rows_of(place)], v_send.at[k * subs + place],
            v_recv.at[k * subs + place], xor(me_row, k, n_row), me_col,
        )

    def pair_copy(j):
        return remote(pair_out.at[j], pair_in.at[j], pair_send.at[j], pair_recv.at[j], me_row, partner)

    def chain_copy(j, h):
        i = j * cuts + h
        return remote(chain_out.at[i], chain_in.at[i], chain_send.at[i], chain_recv.at[i], me_row, inner_col)

    def cross_copy(j, h):
        i = j * cuts + h
        return remote(chain_out.at[i], cross_in.at[i], chain_send.at[i], cross_recv.at[i], me_row, inner_col)

    def far_copy(j, h):
        i, ref = j * cuts + h, rowvals.at[core, j, h * thin:(h + 1) * thin]
        return remote(ref, ref, far_send.at[i], far_recv.at[i], me_row, outer_col)

    def near_copy(j, h):
        i, ref = j * cuts + h, rowvals.at[core, j, h * thin:(h + 1) * thin]
        return remote(ref, ref, near_send.at[i], near_recv.at[i], me_row, partner)

    def part_copy(j):
        return remote(
            part_out.at[j], part_in.at[j], part_send.at[j], part_recv.at[j], xor(me_row, peer_of(j)[0], n_row), me_col
        )

    load_f.wait()

    def build(start, stop):
        @pl.when(active)
        def _():
            @pl.loop(start, stop)
            def _(t):
                at = (t % (n_tiles // 2)) * tile
                count = jnp.broadcast_to(counts_ref[pl.ds(t, 1), :], (tile, tile))
                cols = [
                    jnp.where(s < count, jnp.broadcast_to(cols_ref[pl.ds(t, 1), s:s + 1], (tile, tile)), -1)
                    for s in range(n_slots)
                ]
                for c in range(col_tiles):
                    value = jnp.zeros((tile, tile), jnp.bfloat16)
                    for s in range(n_slots):
                        value = jnp.where(cols[s] == me_col * col_tiles + c, f_all[t, s], value)
                    dense[t // (n_tiles // 2), pl.ds(pl.multiple_of(at, tile), tile), c * tile:(c + 1) * tile] = value

    build(0, n_tiles // 2)

    edges = jnp.where(pair > 0, 1, 0) + jnp.where(pair < n_pair - 1, 1, 0)
    pl.semaphore_wait(barrier, n_row + edges)

    for k in range(1, n_row):
        @pl.when(pair <= last_pair(xor(me_row, k, n_row)))
        def _():
            for place in range(subs):
                v_copy(k, place).start()

    build(n_tiles // 2, n_tiles)
    load_v.wait()

    @pl.when(active)
    def _():
        @pl.loop(0, pieces + final_lag)
        def _(t):
            def valid(j):
                return jnp.logical_and(j >= 0, j < pieces)

            j_total = t - total_lag
            j_in = t - in_lag
            j_out = t - final_lag

            @pl.when(jnp.logical_and(valid(j_total), jnp.logical_not(solo)))
            def _():
                for h in range(cuts):
                    part_rows = slice(h * thin, (h + 1) * thin)

                    @pl.when(center)
                    def _():
                        cross_copy(j_total, h).wait_recv()
                        total = held[j_total, part_rows] + decode(cross_in.at[j_total * cuts + h], thin, half)
                        rowvals[core, j_total, part_rows] = total.astype(jnp.bfloat16)

                    @pl.when(jnp.logical_not(center))
                    def _():
                        far_copy(j_total, h).wait_recv()

                    @pl.when(has_outer)
                    def _():
                        far_copy(j_total, h).start()

                    near_copy(j_total, h).start()

            @pl.when(valid(j_in))
            def _():
                pair_copy(j_in).wait_recv()
                for h in range(cuts):
                    part_rows = slice(h * thin, (h + 1) * thin)
                    held[j_in, part_rows] = own[j_in, part_rows] + pair_in[j_in, part_rows]

                    @pl.when(has_outer)
                    def _():
                        chain_copy(j_in, h).wait_recv()
                        held[j_in, part_rows] += decode(chain_in.at[j_in * cuts + h], thin, half)

                    @pl.when(solo)
                    def _():
                        rowvals[core, j_in, part_rows] = held[j_in, part_rows].astype(jnp.bfloat16)
                        near_copy(j_in, h).start()

                    @pl.when(jnp.logical_not(solo))
                    def _():
                        encode(held[j_in, part_rows], chain_out.at[j_in * cuts + h])

                        @pl.when(center)
                        def _():
                            cross_copy(j_in, h).start()

                        @pl.when(jnp.logical_not(center))
                        def _():
                            chain_copy(j_in, h).start()

            @pl.when(t < pieces)
            def _():
                k, place, is_own = peer_of(t)

                @pl.when(jnp.logical_not(is_own))
                def _():
                    v_copy(k, place).wait_recv()

                vec = v_all[k, rows_of(place), :]
                dims_nt = (((1,), (1,)), ((), ()))
                pair_out[t] = lax.dot_general(vec, dense[1 - core], dims_nt, preferred_element_type=jnp.float32)
                pair_copy(t).start()
                own[t] = lax.dot_general(vec, dense[core], dims_nt, preferred_element_type=jnp.float32)

            @pl.when(valid(j_out))
            def _():
                for h in range(cuts):
                    near_copy(j_out, h).wait_recv()
                part = jnp.dot(rowvals[0, j_out], dense[0], preferred_element_type=jnp.float32)
                part += jnp.dot(rowvals[1, j_out], dense[1], preferred_element_type=jnp.float32)

                k, place, is_own = peer_of(j_out)

                @pl.when(is_own)
                def _():
                    out_ref[rows_of(place), :] = part

                @pl.when(jnp.logical_not(is_own))
                def _():
                    encode(part, part_out.at[j_out])
                    part_copy(j_out).start()

    @pl.when(jnp.logical_not(active))
    def _():
        out_ref[...] = jnp.zeros_like(out_ref)

    @pl.loop(0, pieces)
    def _(j):
        k, place, is_own = peer_of(j)

        @pl.when(jnp.logical_and(jnp.logical_not(is_own), pair <= last_pair(xor(me_row, k, n_row))))
        def _():
            part_copy(j).wait_recv()
            out_ref[rows_of(place), :] += decode(part_in.at[j], rows, width)

    for k in range(1, n_row):
        @pl.when(pair <= last_pair(xor(me_row, k, n_row)))
        def _():
            for place in range(subs):
                v_copy(k, place).wait_send()

    @pl.when(active)
    def _():
        @pl.loop(0, pieces)
        def _(j):
            pair_copy(j).wait_send()
            for h in range(cuts):
                near_copy(j, h).wait_send()

                @pl.when(jnp.logical_not(solo))
                def _():
                    chain_copy(j, h).wait_send()

                @pl.when(has_outer)
                def _():
                    far_copy(j, h).wait_send()

            @pl.when(jnp.logical_not(peer_of(j)[2]))
            def _():
                part_copy(j).wait_send()


def per_device(n_row, n_col, vectors, factor_tiles, tile_columns, live_counts):
    n_tiles, n_slots, tile, _ = factor_tiles.shape
    n_vec, width = vectors.shape
    subs = max(1, n_vec // 64)
    pieces, rows = n_row * subs, n_vec // subs
    half = n_tiles // 2 * tile
    cuts = max(1, min(CUTS, rows // GROUP))
    coded = rows // cuts * half // LANES + GROUP
    thin_pieces = pieces * cuts
    coded_out = rows * width // LANES + GROUP
    dma = pltpu.SemaphoreType.DMA
    return pl.pallas_call(
        functools.partial(kernel, (n_row, n_col, n_tiles, n_slots, tile, width // tile, subs, cuts)),
        out_shape=jax.ShapeDtypeStruct((n_vec, width), jnp.float32),
        in_specs=[
            pl.BlockSpec(memory_space=pltpu.VMEM),
            pl.BlockSpec(memory_space=pltpu.VMEM),
            pl.BlockSpec(memory_space=pl.ANY),
            pl.BlockSpec(memory_space=pl.ANY),
        ],
        out_specs=pl.BlockSpec(memory_space=pltpu.VMEM),
        scratch_shapes=[
            pltpu.VMEM((n_row, n_vec, width), jnp.bfloat16),
            pltpu.VMEM((n_tiles, n_slots, tile, tile), jnp.bfloat16),
            pltpu.VMEM((2, half, width), jnp.bfloat16),
            pltpu.VMEM((pieces, rows, half), jnp.float32),
            pltpu.VMEM((pieces, rows, half), jnp.float32),
            pltpu.VMEM((pieces, rows, half), jnp.float32),
            pltpu.VMEM((pieces, rows, half), jnp.float32),
            pltpu.VMEM((thin_pieces, coded, LANES), jnp.int16),
            pltpu.VMEM((thin_pieces, coded, LANES), jnp.int16),
            pltpu.VMEM((thin_pieces, coded, LANES), jnp.int16),
            pltpu.VMEM((2, pieces, rows, half), jnp.bfloat16),
            pltpu.VMEM((pieces, coded_out, LANES), jnp.int16),
            pltpu.VMEM((pieces, coded_out, LANES), jnp.int16),
            dma((2,)),
            dma((n_row * subs,)), dma((n_row * subs,)),
            dma((pieces,)), dma((pieces,)),
            dma((thin_pieces,)), dma((thin_pieces,)), dma((thin_pieces,)),
            dma((thin_pieces,)), dma((thin_pieces,)),
            dma((thin_pieces,)), dma((thin_pieces,)),
            dma((pieces,)), dma((pieces,)),
        ],
        compiler_params=pltpu.CompilerParams(
            collective_id=0, has_side_effects=True, vmem_limit_bytes=56 * 1024 * 1024
        ),
    )(tile_columns, live_counts, vectors, factor_tiles)


def solution(mesh):
    in_specs = (P("row", "col"), P("row", "col", None, None), P("row", "col"), P("row", "col"))
    out_specs = P("row", "col")
    body = functools.partial(per_device, mesh.shape["row"], mesh.shape["col"])
    return jax.shard_map(body, mesh=mesh, in_specs=in_specs, out_specs=out_specs, check_vma=False)
```

```python
import functools

import jax
import jax.numpy as jnp
from jax import lax
from jax.experimental import pallas as pl
from jax.experimental.pallas import tpu as pltpu
from jax.sharding import PartitionSpec as P

LANES = 128
GROUP = 16
PEAK = 32000.0
CUTS = 1
LAG_PAIR, LAG_IN, LAG_CROSS, LAG_OUT, LAG_NEAR = 1, 2, 2, 2, 1
MESH = pl.DeviceIdType.MESH


def xor(a, b, size):
    both, bit = 0, 1
    while bit < size:
        both = both + bit * ((a // bit) % 2) * ((b // bit) % 2)
        bit *= 2
    return a + b - 2 * both


def encode(value, ref):
    rows, width = value.shape
    most = jnp.full((GROUP, LANES), 1e-30, jnp.float32)
    for at in range(width // LANES):
        part = jnp.abs(value[:, at * LANES:(at + 1) * LANES])
        most = jnp.maximum(most, jnp.max(part.reshape(rows // GROUP, GROUP, LANES), axis=0))
    power = jnp.ceil(jnp.log2(most))
    scale = jnp.tile(jnp.exp2(-power) * PEAK, (rows // GROUP, 1))
    for at in range(width // LANES):
        coded = jnp.round(value[:, at * LANES:(at + 1) * LANES] * scale)
        ref[at * rows:(at + 1) * rows, :] = coded.astype(jnp.int32).astype(jnp.int16)
    ref[rows * width // LANES:, :] = power.astype(jnp.int32).astype(jnp.int16)


def decode(ref, rows, width):
    power = ref[rows * width // LANES:, :].astype(jnp.int32).astype(jnp.float32)
    scale = jnp.tile(jnp.exp2(power) * (1.0 / PEAK), (rows // GROUP, 1))
    parts = [
        ref[at * rows:(at + 1) * rows, :].astype(jnp.int32).astype(jnp.float32) * scale
        for at in range(width // LANES)
    ]
    return jnp.concatenate(parts, axis=1)


def kernel(
    dims, cols_ref, v_hbm, f_hbm, out_ref,
    v_all, f_all, dense, own, pair_out, pair_in, held, chain_out, chain_in, cross_in, rowvals, part_out, part_in,
    load_sem, v_send, v_recv, pair_send, pair_recv, chain_send, chain_recv, cross_recv,
    far_send, far_recv, near_send, near_recv, part_send, part_recv,
):
    n_row, n_col, n_tiles, n_slots, tile, col_tiles, subs, cuts = dims
    n_pair = n_col // 2
    n_vec, width = out_ref.shape
    pieces, rows = n_row * subs, n_vec // subs
    half = n_tiles // 2 * tile
    thin = rows // cuts

    me_row, me_col = lax.axis_index("row"), lax.axis_index("col")
    pair, core = me_col // 2, me_col % 2
    partner = pair * 2 + 1 - core

    def last_pair(row):
        return jnp.minimum(n_pair - 1, ((row + 1) * n_tiles - 1) // (2 * col_tiles))

    last = last_pair(me_row)
    middle = last // 2
    left = pair <= middle
    active = pair <= last
    solo = last == 0
    center = jnp.logical_and(jnp.logical_or(pair == middle, pair == middle + 1), last > 0)
    depth = jnp.where(left, pair, last - pair)
    spread = jnp.where(left, middle - pair, pair - middle - 1)
    has_outer = depth > 0
    outer = jnp.where(left, pair - 1, pair + 1)
    inner = jnp.where(left, pair + 1, pair - 1)
    outer_col, inner_col = outer * 2 + core, inner * 2 + core
    in_lag = LAG_PAIR + LAG_IN * depth
    meet = LAG_PAIR + LAG_IN * jnp.maximum(middle, last - middle - 1) + LAG_CROSS
    total_lag = meet + LAG_OUT * spread
    final_lag = jnp.where(solo, LAG_PAIR, total_lag) + LAG_NEAR

    def peer_of(j):
        others = j - (subs - 1)
        is_last = j == pieces - 1 if subs > 1 else False
        is_own = jnp.logical_or(others < (1 if subs == 1 else 0), is_last)
        place = 0 if subs == 1 else jnp.where(is_last, subs - 1, j)
        shift = others - 1 if subs == 1 else others
        distance = jnp.where(is_own, 0, 1 + shift // subs)
        return distance, jnp.where(is_own, place, shift % subs), is_own

    def rows_of(place):
        return pl.ds(pl.multiple_of(place * rows, rows), rows)

    load_v = pltpu.make_async_copy(v_hbm, v_all.at[0], load_sem.at[0])
    load_f = pltpu.make_async_copy(f_hbm, f_all, load_sem.at[1])
    load_v.start()
    load_f.start()

    barrier = pltpu.get_barrier_semaphore()
    for k in range(1, n_row):
        pl.semaphore_signal(barrier, inc=1, device_id=(xor(me_row, k, n_row), me_col), device_id_type=MESH)
    pl.semaphore_signal(barrier, inc=1, device_id=(me_row, partner), device_id_type=MESH)

    @pl.when(pair > 0)
    def _():
        pl.semaphore_signal(barrier, inc=1, device_id=(me_row, me_col - 2), device_id_type=MESH)

    @pl.when(pair < n_pair - 1)
    def _():
        pl.semaphore_signal(barrier, inc=1, device_id=(me_row, me_col + 2), device_id_type=MESH)

    def remote(src, dst, send, recv, row, col):
        return pltpu.make_async_remote_copy(
            src_ref=src, dst_ref=dst, send_sem=send, recv_sem=recv, device_id=(row, col), device_id_type=MESH
        )

    def v_copy(k, place):
        return remote(
            v_hbm.at[rows_of(place)], v_all.at[k, rows_of(place)], v_send.at[k * subs + place],
            v_recv.at[k * subs + place], xor(me_row, k, n_row), me_col,
        )

    def pair_copy(j):
        return remote(pair_out.at[j], pair_in.at[j], pair_send.at[j], pair_recv.at[j], me_row, partner)

    def chain_copy(j, h):
        i = j * cuts + h
        return remote(chain_out.at[i], chain_in.at[i], chain_send.at[i], chain_recv.at[i], me_row, inner_col)

    def cross_copy(j, h):
        i = j * cuts + h
        return remote(chain_out.at[i], cross_in.at[i], chain_send.at[i], cross_recv.at[i], me_row, inner_col)

    def far_copy(j, h):
        i, ref = j * cuts + h, rowvals.at[core, j, h * thin:(h + 1) * thin]
        return remote(ref, ref, far_send.at[i], far_recv.at[i], me_row, outer_col)

    def near_copy(j, h):
        i, ref = j * cuts + h, rowvals.at[core, j, h * thin:(h + 1) * thin]
        return remote(ref, ref, near_send.at[i], near_recv.at[i], me_row, partner)

    def part_copy(j):
        return remote(
            part_out.at[j], part_in.at[j], part_send.at[j], part_recv.at[j], xor(me_row, peer_of(j)[0], n_row), me_col
        )

    load_f.wait()

    def build(start, stop):
        @pl.when(active)
        def _():
            @pl.loop(start, stop)
            def _(t):
                at = (t % (n_tiles // 2)) * tile
                cols = [
                    jnp.broadcast_to(cols_ref[pl.ds(t, 1), s:s + 1], (tile, tile))
                    for s in range(n_slots)
                ]
                for c in range(col_tiles):
                    value = jnp.zeros((tile, tile), jnp.bfloat16)
                    for s in range(n_slots):
                        value = jnp.where(cols[s] == c, f_all[t, s], value)
                    dense[t // (n_tiles // 2), pl.ds(pl.multiple_of(at, tile), tile), c * tile:(c + 1) * tile] = value

    build(0, n_tiles // 2)

    edges = jnp.where(pair > 0, 1, 0) + jnp.where(pair < n_pair - 1, 1, 0)
    pl.semaphore_wait(barrier, n_row + edges)

    for k in range(1, n_row):
        @pl.when(pair <= last_pair(xor(me_row, k, n_row)))
        def _():
            for place in range(subs):
                v_copy(k, place).start()

    build(n_tiles // 2, n_tiles)
    load_v.wait()

    @pl.when(active)
    def _():
        @pl.loop(0, pieces + final_lag)
        def _(t):
            def valid(j):
                return jnp.logical_and(j >= 0, j < pieces)

            j_total = t - total_lag
            j_in = t - in_lag
            j_out = t - final_lag

            @pl.when(jnp.logical_and(valid(j_total), jnp.logical_not(solo)))
            def _():
                for h in range(cuts):
                    part_rows = slice(h * thin, (h + 1) * thin)

                    @pl.when(center)
                    def _():
                        cross_copy(j_total, h).wait_recv()
                        total = held[j_total, part_rows] + decode(cross_in.at[j_total * cuts + h], thin, half)
                        rowvals[core, j_total, part_rows] = total.astype(jnp.bfloat16)

                    @pl.when(jnp.logical_not(center))
                    def _():
                        far_copy(j_total, h).wait_recv()

                    @pl.when(has_outer)
                    def _():
                        far_copy(j_total, h).start()

                    near_copy(j_total, h).start()

            @pl.when(valid(j_in))
            def _():
                pair_copy(j_in).wait_recv()
                for h in range(cuts):
                    part_rows = slice(h * thin, (h + 1) * thin)
                    held[j_in, part_rows] = own[j_in, part_rows] + pair_in[j_in, part_rows]

                    @pl.when(has_outer)
                    def _():
                        chain_copy(j_in, h).wait_recv()
                        held[j_in, part_rows] += decode(chain_in.at[j_in * cuts + h], thin, half)

                    @pl.when(solo)
                    def _():
                        rowvals[core, j_in, part_rows] = held[j_in, part_rows].astype(jnp.bfloat16)
                        near_copy(j_in, h).start()

                    @pl.when(jnp.logical_not(solo))
                    def _():
                        encode(held[j_in, part_rows], chain_out.at[j_in * cuts + h])

                        @pl.when(center)
                        def _():
                            cross_copy(j_in, h).start()

                        @pl.when(jnp.logical_not(center))
                        def _():
                            chain_copy(j_in, h).start()

            @pl.when(t < pieces)
            def _():
                k, place, is_own = peer_of(t)

                @pl.when(jnp.logical_not(is_own))
                def _():
                    v_copy(k, place).wait_recv()

                vec = v_all[k, rows_of(place), :]
                dims_nt = (((1,), (1,)), ((), ()))
                pair_out[t] = lax.dot_general(vec, dense[1 - core], dims_nt, preferred_element_type=jnp.float32)
                pair_copy(t).start()
                own[t] = lax.dot_general(vec, dense[core], dims_nt, preferred_element_type=jnp.float32)

            @pl.when(valid(j_out))
            def _():
                for h in range(cuts):
                    near_copy(j_out, h).wait_recv()
                part = jnp.dot(rowvals[0, j_out], dense[0], preferred_element_type=jnp.float32)
                part += jnp.dot(rowvals[1, j_out], dense[1], preferred_element_type=jnp.float32)

                k, place, is_own = peer_of(j_out)

                @pl.when(is_own)
                def _():
                    out_ref[rows_of(place), :] = part

                @pl.when(jnp.logical_not(is_own))
                def _():
                    encode(part, part_out.at[j_out])
                    part_copy(j_out).start()

    @pl.when(jnp.logical_not(active))
    def _():
        out_ref[...] = jnp.zeros_like(out_ref)

    @pl.loop(0, pieces)
    def _(j):
        k, place, is_own = peer_of(j)

        @pl.when(jnp.logical_and(jnp.logical_not(is_own), pair <= last_pair(xor(me_row, k, n_row))))
        def _():
            part_copy(j).wait_recv()
            out_ref[rows_of(place), :] += decode(part_in.at[j], rows, width)

    for k in range(1, n_row):
        @pl.when(pair <= last_pair(xor(me_row, k, n_row)))
        def _():
            for place in range(subs):
                v_copy(k, place).wait_send()

    @pl.when(active)
    def _():
        @pl.loop(0, pieces)
        def _(j):
            pair_copy(j).wait_send()
            for h in range(cuts):
                near_copy(j, h).wait_send()

                @pl.when(jnp.logical_not(solo))
                def _():
                    chain_copy(j, h).wait_send()

                @pl.when(has_outer)
                def _():
                    far_copy(j, h).wait_send()

            @pl.when(jnp.logical_not(peer_of(j)[2]))
            def _():
                part_copy(j).wait_send()


def per_device(n_row, n_col, vectors, factor_tiles, tile_columns, live_counts):
    n_tiles, n_slots, tile, _ = factor_tiles.shape
    n_vec, width = vectors.shape
    subs = max(1, n_vec // 64)
    pieces, rows = n_row * subs, n_vec // subs
    half = n_tiles // 2 * tile
    cuts = max(1, min(CUTS, rows // GROUP))
    coded = rows // cuts * half // LANES + GROUP
    thin_pieces = pieces * cuts
    coded_out = rows * width // LANES + GROUP
    dma = pltpu.SemaphoreType.DMA
    slot = lax.broadcasted_iota(jnp.int32, tile_columns.shape, 1)
    places = jnp.where(slot < live_counts, tile_columns - lax.axis_index("col") * (width // tile), -1)
    return pl.pallas_call(
        functools.partial(kernel, (n_row, n_col, n_tiles, n_slots, tile, width // tile, subs, cuts)),
        out_shape=jax.ShapeDtypeStruct((n_vec, width), jnp.float32),
        in_specs=[
            pl.BlockSpec(memory_space=pltpu.VMEM),
            pl.BlockSpec(memory_space=pl.ANY),
            pl.BlockSpec(memory_space=pl.ANY),
        ],
        out_specs=pl.BlockSpec(memory_space=pltpu.VMEM),
        scratch_shapes=[
            pltpu.VMEM((n_row, n_vec, width), jnp.bfloat16),
            pltpu.VMEM((n_tiles, n_slots, tile, tile), jnp.bfloat16),
            pltpu.VMEM((2, half, width), jnp.bfloat16),
            pltpu.VMEM((pieces, rows, half), jnp.float32),
            pltpu.VMEM((pieces, rows, half), jnp.float32),
            pltpu.VMEM((pieces, rows, half), jnp.float32),
            pltpu.VMEM((pieces, rows, half), jnp.float32),
            pltpu.VMEM((thin_pieces, coded, LANES), jnp.int16),
            pltpu.VMEM((thin_pieces, coded, LANES), jnp.int16),
            pltpu.VMEM((thin_pieces, coded, LANES), jnp.int16),
            pltpu.VMEM((2, pieces, rows, half), jnp.bfloat16),
            pltpu.VMEM((pieces, coded_out, LANES), jnp.int16),
            pltpu.VMEM((pieces, coded_out, LANES), jnp.int16),
            dma((2,)),
            dma((n_row * subs,)), dma((n_row * subs,)),
            dma((pieces,)), dma((pieces,)),
            dma((thin_pieces,)), dma((thin_pieces,)), dma((thin_pieces,)),
            dma((thin_pieces,)), dma((thin_pieces,)),
            dma((thin_pieces,)), dma((thin_pieces,)),
            dma((pieces,)), dma((pieces,)),
        ],
        compiler_params=pltpu.CompilerParams(
            collective_id=0, has_side_effects=True, vmem_limit_bytes=56 * 1024 * 1024
        ),
    )(places, vectors, factor_tiles)


def solution(mesh):
    in_specs = (P("row", "col"), P("row", "col", None, None), P("row", "col"), P("row", "col"))
    out_specs = P("row", "col")
    body = functools.partial(per_device, mesh.shape["row"], mesh.shape["col"])
    return jax.shard_map(body, mesh=mesh, in_specs=in_specs, out_specs=out_specs, check_vma=False)
```
